256 devices in a mesh: dp: 64 (over z, x_hi, y), mp: 4 (over x_lo, core).
Axes of the slice: x: 4 (x_hi: 2, x_lo: 2; x = x_hi * 2 + x_lo), y: 4, z: 8, core: 2. Of those that a mesh axis runs over, the one named last changes fastest.
Arguments:
- proxy_loss: float32 [49152], P(('dp', 'mp')), may hold values from 0.3 to 7
- ref_loss: float32 [49152], P(('dp', 'mp')), may hold values from 1 to 4
- domain_ids: int32 [49152], P(('dp', 'mp')), may hold values from 0 to 63, as said below
- prev_weights: float32 [64], replicated, may hold values from 0.005 to 0.05
- attn_context: bfloat16 [49152, 4096], P('dp', 'mp'), may hold values from -6 to 6
- out_weight: bfloat16 [4096, 4096], P(None, 'mp'), may hold values from -0.09375 to 0.09375
- layer_cot: bfloat16 [49152, 4096], P(('dp', 'mp')), may hold values from -24 to 24
Outputs:
- domain_weights: float32 [64], replicated
- context_grad: bfloat16 [49152, 4096], P('dp', 'mp')
- weight_grad: float32 [4096, 4096], P('dp', 'mp')
The draws below stay inside these ranges and needn't reach their ends.
Inputs may be any that keep to these rules, and one draw needn't show every extreme that they name: `domain_ids`: any domain id of 0 .. 63 may occur, and some domains may have no tokens at all; both ends occur in every draw.
All inputs are finite; a program needn't handle non-finite values.
Results may differ from the reference program's by a relative error of at most 0.0049.
Values may be sent and summed in bfloat16 or wider, within the bound.
No kernel may reach another device: no remote copies, remote signals or barrier semaphores. Data moves between devices by JAX's collectives and lax.ppermute only.
A program may use at most 128 MiB of HBM per device.

```python
import math
import jax
import jax.numpy as jnp
from jax import lax

D = 4096
DOMAINS = 64
TOKENS = 49152


def domain_labels(key):
    folded = jax.random.fold_in(key, 7)
    key_one, key_two, key_three, key_four, key_five = jax.random.split(folded, 5)
    draw_one = jax.random.randint(key_one, (TOKENS,), 0, DOMAINS)
    draw_two = jax.random.randint(key_two, (TOKENS,), 0, DOMAINS)
    draw_three = jax.random.randint(key_three, (TOKENS,), 0, DOMAINS)
    position = jnp.arange(TOKENS, dtype=jnp.int32)
    choose_min = jax.random.randint(key_four, (TOKENS,), 0, TOKENS) < position
    labels = jnp.where(choose_min, jnp.minimum(draw_one, jnp.minimum(draw_two, draw_three)), draw_one)
    emptied = jax.random.permutation(key_five, DOMAINS - 2)[:4] + 1
    is_emptied = jnp.any(labels[:, None] == emptied[None, :], axis=1)
    labels = jnp.where(is_emptied, 0, labels)
    labels = labels.at[0].set(DOMAINS - 1).at[1].set(0)
    return labels.astype(jnp.int32)


def loss_pair(key):
    labels = domain_labels(key)
    key_ref, key_table, key_jitter = jax.random.split(jax.random.fold_in(key, 23), 3)
    ref_values = jax.random.uniform(key_ref, (TOKENS,), jnp.float32, 1.0, 4.0)
    offset = jax.random.uniform(key_table, (DOMAINS,), jnp.float32, -0.3, 0.3)
    jitter = jax.random.uniform(key_jitter, (TOKENS,), jnp.float32, -0.5, 0.5)
    fraction = jnp.arange(TOKENS).astype(jnp.float32) / TOKENS
    growth = 0.5 + fraction
    proxy_values = ref_values + (0.5 + offset[labels] + jitter) * growth
    return (ref_values, proxy_values)


def draw_domain_ids(key, part):
    return domain_labels(key)


def draw_ref_loss(key, part):
    return loss_pair(key)[0].astype(jnp.float32)


def draw_proxy_loss(key, part):
    return loss_pair(key)[1].astype(jnp.float32)


def strengthened(array, rng, source, target, shards_of, factor):
    owner, partner = [(jnp.arange(array.shape[dim]) // (array.shape[dim] // shards_of)).reshape([-1 if axis == dim else 1 for axis in range(array.ndim)]) for dim in (source, target)]
    chosen = jax.random.permutation(rng, shards_of)[partner]
    strong = (owner == chosen) | (owner == (partner + shards_of // 2) % shards_of)
    return jnp.where(strong, factor * array, array)


def levels(own_key, extent, pieces, least, high):
    def one(dim, blocks):
        steps = jax.random.uniform(jax.random.fold_in(jax.random.fold_in(own_key, 6), dim), (blocks,), jnp.float32, least / len(pieces), high / len(pieces))
        return jnp.repeat(jnp.exp(steps), extent[dim] // blocks).reshape((-1,) + (1,) * (len(extent) - dim - 1))

    level = one(*pieces[0])
    for cut in pieces[1:]:
        level = level * one(*cut)
    return level


def centred(key, dims, spread, most, pieces=(), kind=jnp.bfloat16):
    factor_of = levels(key, dims, pieces, -0.22, 0.18) if pieces else 1.0
    result = jax.random.normal(key, dims, jnp.float32) * spread * factor_of
    return jnp.minimum(jnp.maximum(result, -most), most).astype(kind)


def bell_draw_with(own_key, dims, spread, most, shards, heavy, kind=jnp.bfloat16):
    array = spread * jax.random.normal(own_key, dims, jnp.float32)
    if shards:
        array = array * levels(own_key, dims, shards, -0.22, 0.18)
    return jnp.clip(strengthened(array, jax.random.fold_in(own_key, 3), *heavy), -most, most).astype(kind)


def setup_inputs(seed: int = 0) -> dict:
    keys = jax.random.split(jax.random.key(seed), 8)
    return {
        "proxy_loss": draw_proxy_loss(jax.random.fold_in(keys[7], 71), 0),
        "ref_loss": draw_ref_loss(jax.random.fold_in(keys[7], 71), 0),
        "domain_ids": draw_domain_ids(jax.random.fold_in(keys[7], 71), 0),
        "prev_weights": jnp.clip(jnp.exp(jax.random.uniform(keys[3], (DOMAINS,), jnp.float32, math.log(0.005), math.log(0.05))), 0.005, 0.05),
        "attn_context": centred(keys[4], (TOKENS, D), 1.0, 6.0, ((0, 64), (1, 4))),
        "out_weight": centred(keys[5], (D, D), D ** -0.5, 0.09375, ((1, 4),)),
        "layer_cot": bell_draw_with(keys[6], (TOKENS, D), 1.0, 24.0, ((0, 256),), (0, 1, 256, 6.0)),
    }


step_size = 1.0
smoothing = 0.001

def reference(proxy_loss, ref_loss, domain_ids, prev_weights, attn_context, out_weight, layer_cot):
    excess = jnp.maximum(proxy_loss - ref_loss, 0.0)
    labels = jnp.arange(DOMAINS, dtype=jnp.int32)
    onehot = (domain_ids[:, None] == labels[None, :]).astype(jnp.float32)
    totals = jnp.dot(excess, onehot, precision=lax.Precision.HIGHEST)
    counts = lax.optimization_barrier(jnp.sum(onehot, axis=0))
    denominator = jnp.maximum(counts, 1.0)
    unnormed = prev_weights * jnp.exp(step_size * totals / denominator)
    mixture = (1.0 - smoothing) * unnormed / jnp.sum(unnormed) + smoothing / DOMAINS
    domain_scale = mixture * TOKENS / denominator
    token_scale = jnp.dot(onehot, domain_scale, precision=lax.Precision.HIGHEST)
    weighted = (token_scale[:, None] * layer_cot.astype(jnp.float32)).astype(jnp.bfloat16)
    context_grad = jnp.dot(weighted, out_weight, preferred_element_type=jnp.float32).astype(jnp.bfloat16)
    weight_grad = lax.dot_general(weighted, attn_context, (((0,), (0,)), ((), ())), preferred_element_type=jnp.float32)
    weight_grad = weight_grad * (1.0 / math.sqrt(TOKENS))
    return (mixture, context_grad, weight_grad)
```

```python
import functools

import jax
import jax.numpy as jnp
from jax import lax
from jax.experimental import pallas as pl
from jax.experimental.pallas import tpu as pltpu
from jax.sharding import Mesh
from jax.sharding import PartitionSpec as P

DP = ("z", "xh", "y")
ALL = ("z", "xh", "y", "xl", "c")
MP = ("xl", "c")
step_size = 1.0
smoothing = 0.001
BF = jnp.bfloat16
F32 = jnp.float32
ROWS = 192
COLS = 1024
HALF = 2048
CUT = 384


def swap(x, axis, by=1):
    return lax.ppermute(x, axis, [(i, i ^ by) for i in range(lax.axis_size(axis))])


def shift(x, axis, by):
    n = lax.axis_size(axis)
    return lax.ppermute(x, axis, [(i, (i + by) % n) for i in range(n)])


def ring_sum(x, axis):
    n = lax.axis_size(axis)
    far = n // 2
    up, down = x[far, :1], x[far, 1:]
    for step in range(1, far + 1):
        up, down = shift(up, axis, 1).astype(F32), shift(down, axis, -1).astype(F32)
        if step == far:
            return x[0].astype(F32) + up + down
        a, b = x[far - step].astype(F32), x[n - far + step].astype(F32)
        if step == 1:
            up = jnp.concatenate([a[:1] + up, a[1:]], 0).astype(BF)
            down = jnp.concatenate([b[:1], b[1:] + down], 0).astype(BF)
        else:
            up, down = (a + up).astype(BF), (b + down).astype(BF)


def everyones(x, axes):
    n = lax.axis_size(axes)
    return lax.all_to_all(jnp.broadcast_to(x, (n, *x.shape)), axes, 0, 0, tiled=True)


def split_kernel(info, x, home, away):
    for t in range(4):
        at = pl.multiple_of(info[2] * 128, 128)
        home[:, t * 128 : t * 128 + 128] = x[:, pl.ds(t * 256 + at, 128)]
        away[:, t * 128 : t * 128 + 128] = x[:, pl.ds(t * 256 + (128 - at), 128)]


def split_features(info, cot):
    out = jax.ShapeDtypeStruct((ROWS, HALF), BF)
    return pl.pallas_call(
        split_kernel,
        out_shape=(out, out),
        grid_spec=pltpu.PrefetchScalarGridSpec(
            num_scalar_prefetch=1,
            grid=(4,),
            in_specs=[pl.BlockSpec((ROWS, 1024), lambda i, s: (0, i))],
            out_specs=[pl.BlockSpec((ROWS, 512), lambda i, s: (0, i))] * 2,
        ),
        cost_estimate=pl.CostEstimate(flops=0, bytes_accessed=3 << 20, transcendentals=0),
        name="split",
    )(info, cot)


def outer_kernel(info, *refs):
    cots, (ctx, far_ctx, scale) = refs[:8], refs[8:11]
    keep, send, rest, scaled, acc = refs[11:]

    @pl.when(pl.program_id(0) == 0)
    def _():
        for g, source in enumerate((ctx, far_ctx)):
            for k in range(4):
                at = pl.multiple_of((info[0] ^ k) * ROWS, ROWS)
                weigh = scale[pl.ds(g * 768 + at, ROWS), :] * (49152.0**-0.5)
                rows = source[pl.ds(at, ROWS), :].astype(F32) * weigh
                scaled[(g * 4 + k) * ROWS : (g * 4 + k + 1) * ROWS, :] = rows.astype(BF)

    lhs = jnp.concatenate([c[...] for c in cots], 0)
    acc[...] = lax.dot_general(
        lhs, scaled[...], (((0,), (0,)), ((), ())), preferred_element_type=F32
    )
    for h in range(2):
        for p in range(2):
            at = pl.multiple_of((info[4] ^ h) * 128 + (info[3] ^ p) * 64, 64)
            rows = acc[pl.ds(at, 64), :].astype(BF)
            (keep, send)[p][0, h] = rows[:, :CUT]
            rest[0, p, h * 64 : h * 64 + 64] = rows[:, CUT:]


def outer_product(info, cots, ctx, far_ctx, scale):
    turned = lambda i, s: ((i - s[1]) & 7, 0, 0, 0)
    one = jax.ShapeDtypeStruct((8, 2, 64, CUT), BF)
    return pl.pallas_call(
        outer_kernel,
        out_shape=(one, one, jax.ShapeDtypeStruct((8, 2, 128, COLS - CUT), BF)),
        grid_spec=pltpu.PrefetchScalarGridSpec(
            num_scalar_prefetch=1,
            grid=(8,),
            in_specs=[pl.BlockSpec((ROWS, 256), lambda i, s: (0, i))] * 8
            + [pl.BlockSpec((768, COLS), lambda i, s: (0, 0), pipeline_mode=pl.Buffered(1))] * 2
            + [pl.BlockSpec((1536, 1), lambda i, s: (0, 0), pipeline_mode=pl.Buffered(1))],
            out_specs=[pl.BlockSpec((1, 2, 64, CUT), turned)] * 2
            + [pl.BlockSpec((1, 2, 128, COLS - CUT), turned)],
            scratch_shapes=[pltpu.VMEM((1536, COLS), BF), pltpu.VMEM((256, COLS), F32)],
        ),
        cost_estimate=pl.CostEstimate(flops=2 * 1536 * 2048 * 1024, bytes_accessed=14 << 20, transcendentals=0),
        compiler_params=pltpu.CompilerParams(vmem_limit_bytes=32 << 20),
        name="outer",
    )(info, *cots, ctx, far_ctx, scale)


def context_kernel(info, *refs):
    homes, aways, (weight, scale, out, acc) = refs[:4], refs[4:8], refs[8:]
    step = pl.program_id(0)

    @pl.when(step == 0)
    def _():
        acc[...] = jnp.zeros_like(acc)

    at = pl.multiple_of(info[2] * 128, 128)
    total = acc[...]
    for blocks, off in ((homes, at), (aways, 128 - at)):
        lhs = jnp.concatenate([b[...] for b in blocks], 0)
        w = jnp.concatenate([weight[pl.ds(off, 128), :], weight[pl.ds(256 + off, 128), :]], 0)
        total = total + jnp.dot(lhs, w, preferred_element_type=F32)
    acc[...] = total

    @pl.when(step == pl.num_programs(0) - 1)
    def _():
        for k in range(4):
            at = pl.multiple_of((info[0] ^ k) * ROWS, ROWS)
            rows = acc[k * ROWS : (k + 1) * ROWS, :] * scale[pl.ds(at, ROWS), :]
            out[pl.ds(at, ROWS), :] = rows.astype(BF)


def context_product(info, homes, aways, weight, scale):
    return pl.pallas_call(
        context_kernel,
        out_shape=jax.ShapeDtypeStruct((768, COLS), BF),
        grid_spec=pltpu.PrefetchScalarGridSpec(
            num_scalar_prefetch=1,
            grid=(8,),
            in_specs=[pl.BlockSpec((ROWS, 256), lambda i, s: (0, i))] * 8
            + [pl.BlockSpec((512, COLS), lambda i, s: (i, 0))]
            + [pl.BlockSpec((768, 1), lambda i, s: (0, 0), pipeline_mode=pl.Buffered(1))],
            out_specs=pl.BlockSpec((768, COLS), lambda i, s: (0, 0)),
            scratch_shapes=[pltpu.VMEM((768, COLS), F32)],
        ),
        cost_estimate=pl.CostEstimate(flops=2 * 768 * 4096 * 1024, bytes_accessed=16 << 20, transcendentals=0),
        compiler_params=pltpu.CompilerParams(vmem_limit_bytes=32 << 20),
        name="context",
    )(info, *homes, *aways, weight, scale)


def shards(proxy_loss, ref_loss, domain_ids, prev_weights, attn_context, out_weight, layer_cot):
    domains = prev_weights.shape[0]
    tokens = layer_cot.shape[0] * 256
    z, xh, y = (lax.axis_index(a) for a in DP)
    info = jnp.stack([lax.axis_index(MP), z, y // 2, y % 2, xh]).astype(jnp.int32)

    home, away = split_features(info, layer_cot)
    far_home = swap(away, "y", 2)

    table = jnp.arange(domains, dtype=jnp.int32).astype(F32)
    excess = jnp.maximum(proxy_loss - ref_loss, 0.0)
    labels = domain_ids.astype(F32)
    onehot = labels[:, None] == table[None, :]
    totals = jnp.sum(jnp.where(onehot, excess[:, None], 0.0), 0)
    counts = jnp.sum(onehot.astype(F32), 0)
    line = jnp.concatenate([totals, counts, labels, jnp.zeros((64,), F32)])
    line = everyones(line[None], ("xh", "xl", "c")).reshape(8, -1)
    home, away, far_home, line = lax.optimization_barrier((home, away, far_home, line))
    stats = jnp.sum(line[:, :128], 0)
    labels = lax.dynamic_slice_in_dim(line[:, 128:320], xh * 4, 4, 0).reshape(-1)
    x_home = swap(home, "xl")
    line = everyones(jnp.concatenate([stats, labels])[None], "y").reshape(4, -1)
    far_home, attn_context, line = lax.optimization_barrier((far_home, attn_context, line))
    x_far = swap(far_home, "xl")
    far_context = swap(attn_context, "y", 2)
    stats = jnp.sum(line[:, :128], 0)
    far_labels = lax.dynamic_index_in_dim(line[:, 128:], y ^ 2, 0, keepdims=False)
    stats = jnp.sum(everyones(stats[None], "z").reshape(8, -1), 0)
    x_far, away, stats = lax.optimization_barrier((x_far, away, stats))

    totals, counts = stats[:domains], stats[domains:]
    denominator = jnp.maximum(counts, 1.0)
    unnormed = prev_weights * jnp.exp(step_size * totals / denominator)
    mixture = (1.0 - smoothing) * unnormed / jnp.sum(unnormed) + smoothing / domains
    scale_table = mixture * tokens / denominator
    onehot = jnp.concatenate([labels, far_labels])[:, None] == table[None, :]
    scale = jnp.sum(jnp.where(onehot, scale_table[None, :], 0.0), -1, keepdims=True)

    cots = [home, swap(home, "c"), x_home, swap(x_home, "c")]
    far_cots = [far_home, swap(far_home, "c"), x_far, swap(x_far, "c")]
    keep, send, rest = outer_product(info, cots + far_cots, attn_context, far_context, scale)

    got = swap(send, "y", 1)
    first = ring_sum((keep.astype(F32) + got.astype(F32)).astype(BF), "z")
    second = ring_sum(rest, "z")
    second = second[0] + swap(second[1].astype(BF), "y", 1).astype(F32)
    both = jnp.concatenate([first, second.reshape(2, 64, -1)], -1)
    weight_grad = both[0] + swap(both[1].astype(BF), "xh").astype(F32)

    x_away = swap(away, "xl")
    aways = [away, swap(away, "c"), x_away, swap(x_away, "c")]
    grad = context_product(info, cots, aways, out_weight, scale[:768])
    return mixture, grad, weight_grad


def solution(mesh):
    split = Mesh(mesh.devices.reshape(8, 2, 4, 2, 2), ALL)
    placed = (P(ALL), P(ALL), P(ALL), P(), P(DP, MP), P(None, MP), P(ALL, None))
    return jax.shard_map(
        shards,
        mesh=split,
        in_specs=placed,
        out_specs=(P(), P(DP, MP), P(DP, MP)),
        check_vma=False,
    )
```

```python
import jax
import jax.numpy as jnp
from jax import lax
from jax.experimental import pallas as pl
from jax.experimental.pallas import tpu as pltpu
from jax.sharding import Mesh
from jax.sharding import PartitionSpec as P


DP = ("z", "xh", "y")
ALL = ("z", "xh", "y", "xl", "c")
MP = ("xl", "c")
step_size = 1.0
smoothing = 0.001
BF = jnp.bfloat16
F32 = jnp.float32
ROWS = 192
COLS = 1024
HALF = 2048
REST = 512
SIDE = 256


def swap(x, axis, by=1):
    return lax.ppermute(x, axis, [(i, i ^ by) for i in range(lax.axis_size(axis))])


def shift(x, axis, by):
    n = lax.axis_size(axis)
    return lax.ppermute(x, axis, [(i, (i + by) % n) for i in range(n)])


def ring_sum(x, axis):
    n = lax.axis_size(axis)
    far = n // 2
    up, down = x[far], None
    for step in range(1, far + 1):
        up = shift(up, axis, 1).astype(F32)
        if step > 1:
            down = shift(down, axis, -1).astype(F32)
        if step == far:
            return x[0].astype(F32) + up + down
        up = (x[far - step].astype(F32) + up).astype(BF)
        after = x[n - far + step]
        down = after if step == 1 else (after.astype(F32) + down).astype(BF)


def everyones(x, axes):
    n = lax.axis_size(axes)
    return lax.all_to_all(jnp.broadcast_to(x, (n, *x.shape)), axes, 0, 0, tiled=True)


def split_kernel(info, x, home, away):
    for t in range(4):
        at = pl.multiple_of(info[2] * 128, 128)
        home[:, t * 128 : t * 128 + 128] = x[:, pl.ds(t * 256 + at, 128)]
        away[:, t * 128 : t * 128 + 128] = x[:, pl.ds(t * 256 + (128 - at), 128)]


def split_features(info, cot):
    out = jax.ShapeDtypeStruct((ROWS, HALF), BF)
    return pl.pallas_call(
        split_kernel,
        out_shape=(out, out),
        grid_spec=pltpu.PrefetchScalarGridSpec(
            num_scalar_prefetch=1,
            grid=(4,),
            in_specs=[pl.BlockSpec((ROWS, 1024), lambda i, s: (0, i))],
            out_specs=[pl.BlockSpec((ROWS, 512), lambda i, s: (0, i))] * 2,
        ),
        cost_estimate=pl.CostEstimate(flops=0, bytes_accessed=3 << 20, transcendentals=0),
        name="split",
    )(info, cot)


def scaled_rows(info, k, source, scale):
    at = pl.multiple_of((info[0] ^ k) * ROWS, ROWS)
    weigh = scale[pl.ds(at, ROWS), :] * (49152.0**-0.5)
    return (source[pl.ds(at, ROWS), :].astype(F32) * weigh).astype(BF)


def pick(info, ref):
    at = pl.multiple_of(info[2] * 128, 128)
    return jnp.concatenate([ref[:, pl.ds(at, 128)], ref[:, pl.ds(256 + at, 128)]], 1)


def product(lhs, rhs):
    return lax.dot_general(lhs, rhs, (((0,), (0,)), ((), ())), preferred_element_type=F32)


def whole(*shape):
    return pl.BlockSpec(shape, lambda i, s: (0,) * len(shape), pipeline_mode=pl.Buffered(1))


def outer_kernel(info, *refs):
    cots, (ctx, far_ctx, scale, far_scale) = refs[:8], refs[8:12]
    rest, kept_y, sent_y, kept_x, sent_x, scaled, acc = refs[12:]

    @pl.when(pl.program_id(0) == 0)
    def _():
        for g, (source, weigh) in enumerate(((ctx, scale), (far_ctx, far_scale))):
            for k in range(4):
                n = g * 4 + k
                scaled[n * ROWS : (n + 1) * ROWS, :] = scaled_rows(info, k, source, weigh)

    lhs = jnp.concatenate([pick(info, c) for c in cots[:2]] + [c[...] for c in cots[2:]], 0)
    acc[...] = product(lhs, scaled[...])
    for h in range(2):
        for p in range(2):
            at = pl.multiple_of((info[4] ^ h) * 128 + (info[3] ^ p) * 64, 64)
            rows = acc[pl.ds(at, 64), :].astype(BF)
            rest[0, p, h * 64 : h * 64 + 64] = rows[:, :REST]
            (kept_y, sent_y)[p][0, h] = rows[:, REST : REST + SIDE]
            (kept_x, sent_x)[h][0, p] = rows[:, REST + SIDE :]


def outer(info, cots, ctx, far_ctx, scale, far_scale):
    turned = lambda i, s: ((i - s[1]) & 7, 0, 0, 0)
    shapes = [(2, 128, REST)] + [(2, 64, SIDE)] * 2 + [(2, 64, COLS - REST - SIDE)] * 2
    return pl.pallas_call(
        outer_kernel,
        out_shape=[jax.ShapeDtypeStruct((8, *shape), BF) for shape in shapes],
        grid_spec=pltpu.PrefetchScalarGridSpec(
            num_scalar_prefetch=1,
            grid=(8,),
            in_specs=[pl.BlockSpec((ROWS, 512), lambda i, s: (0, i))] * 2
            + [pl.BlockSpec((ROWS, 256), lambda i, s: (0, i))] * 6
            + [whole(768, COLS)] * 2
            + [whole(768, 1)] * 2,
            out_specs=[pl.BlockSpec((1, *shape), turned) for shape in shapes],
            scratch_shapes=[pltpu.VMEM((8 * ROWS, COLS), BF), pltpu.VMEM((256, COLS), F32)],
        ),
        cost_estimate=pl.CostEstimate(flops=2 * 1536 * 2048 * 1024, bytes_accessed=14 << 20, transcendentals=0),
        name="outer",
    )(info, *cots, ctx, far_ctx, scale, far_scale)


def accumulate(acc, value):
    step = pl.program_id(0)

    @pl.when(step == 0)
    def _():
        acc[...] = value

    @pl.when(step > 0)
    def _():
        acc[...] += value


def context_near_kernel(info, own, core, weight, out):
    lhs = jnp.concatenate([own[...], core[...]], 0)
    accumulate(out, jnp.dot(lhs, weight[...], preferred_element_type=F32))


def half_weight(info, weight, away):
    at = pl.multiple_of(info[2] * 128, 128)
    at = 128 - at if away else at
    return jnp.concatenate([weight[pl.ds(at, 128), :], weight[pl.ds(256 + at, 128), :]], 0)


def context_home_kernel(info, x, x_core, weight, out):
    lhs = jnp.concatenate([x[...], x_core[...]], 0)
    accumulate(out, jnp.dot(lhs, half_weight(info, weight, False), preferred_element_type=F32))


def context_last_kernel(info, x, x_core, weight, near, part, scale, out, acc):
    lhs = jnp.concatenate([x[...], x_core[...]], 0)
    accumulate(acc, jnp.dot(lhs, half_weight(info, weight, True), preferred_element_type=F32))

    @pl.when(pl.program_id(0) == pl.num_programs(0) - 1)
    def _():
        for k in range(4):
            at = pl.multiple_of((info[0] ^ k) * ROWS, ROWS)
            rows = slice((k % 2) * ROWS, (k % 2 + 1) * ROWS)
            value = near[rows, :] if k < 2 else acc[rows, :] + part[rows, :]
            out[pl.ds(at, ROWS), :] = (value * scale[pl.ds(at, ROWS), :]).astype(BF)


def context_call(kernel, info, blocks, weight, rest=(), width=256):
    last = bool(rest)
    return pl.pallas_call(
        kernel,
        out_shape=jax.ShapeDtypeStruct((768, COLS), BF) if last else jax.ShapeDtypeStruct((384, COLS), F32),
        grid_spec=pltpu.PrefetchScalarGridSpec(
            num_scalar_prefetch=1,
            grid=(8,),
            in_specs=[pl.BlockSpec((ROWS, width), lambda i, s: (0, i))] * 2
            + [pl.BlockSpec((512, COLS), lambda i, s: (i, 0))]
            + [whole(*r.shape) for r in rest],
            out_specs=pl.BlockSpec((768, COLS) if last else (384, COLS), lambda i, s: (0, 0)),
            scratch_shapes=[pltpu.VMEM((384, COLS), F32)] if last else [],
        ),
        compiler_params=pltpu.CompilerParams(vmem_limit_bytes=(24 if last else 60) << 20),
        cost_estimate=pl.CostEstimate(flops=2 * 384 * 8 * width * 1024, bytes_accessed=8 << 20, transcendentals=0),
    )(info, *blocks, weight, *rest)


def work(proxy_loss, ref_loss, domain_ids, prev_weights, attn_context, out_weight, layer_cot):
    domains = prev_weights.shape[0]
    tokens = layer_cot.shape[0] * 256
    z, xh, y = (lax.axis_index(a) for a in DP)
    info = jnp.stack([lax.axis_index(MP), z, y // 2, y % 2, xh]).astype(jnp.int32)

    table = jnp.arange(domains, dtype=jnp.int32).astype(F32)
    excess = jnp.maximum(proxy_loss - ref_loss, 0.0)
    labels = domain_ids.astype(F32)
    onehot = labels[:, None] == table[None, :]
    totals = jnp.sum(jnp.where(onehot, excess[:, None], 0.0), 0)
    counts = jnp.sum(onehot.astype(F32), 0)
    line = jnp.concatenate([totals, counts, labels, jnp.zeros((64,), F32)])
    line = everyones(line[None], "y").reshape(4, -1)
    home, away = split_features(info, layer_cot)
    core = swap(layer_cot, "c", 1)
    line, rest_ctx = lax.optimization_barrier((line, attn_context))
    far = swap(away, "y", 2)
    stats = jnp.sum(line[:, :128], 0)
    far_labels = lax.dynamic_index_in_dim(line[:, 128:320], y ^ 2, 0, keepdims=False)
    line = everyones(jnp.concatenate([stats, labels, far_labels])[None], ("xh", "xl", "c")).reshape(8, -1)
    near = context_call(context_near_kernel, info, (layer_cot, core), out_weight, width=512)
    x = swap(home, "xl", 1)
    stats = jnp.sum(line[:, :128], 0)
    group = lax.dynamic_slice_in_dim(line[:, 128:], xh * 4, 4, 0)
    labels, far_labels = group[:, :192].reshape(-1), group[:, 192:].reshape(-1)
    stats = jnp.sum(everyones(stats[None], "z").reshape(8, -1), 0)
    x_far = swap(far, "xl", 1)
    far_context = swap(rest_ctx, "y", 2)

    totals, counts = stats[:domains], stats[domains:]
    denominator = jnp.maximum(counts, 1.0)
    unnormed = prev_weights * jnp.exp(step_size * totals / denominator)
    mixture = (1.0 - smoothing) * unnormed / jnp.sum(unnormed) + smoothing / domains
    scale_table = mixture * tokens / denominator

    def scale_of(labels):
        onehot = labels[:, None] == table[None, :]
        return jnp.sum(jnp.where(onehot, scale_table[None, :], 0.0), -1, keepdims=True)

    scale, far_scale = scale_of(labels), scale_of(far_labels)
    far_core, x_core = swap(far, "c"), swap(x, "c")
    part = context_call(context_home_kernel, info, (x, x_core), out_weight)
    x_far, away, part = lax.optimization_barrier((x_far, away, part))
    x_away = swap(away, "xl", 1)
    cots = [layer_cot, core, x, x_core, far, far_core, x_far, swap(x_far, "c")]
    rest, kept_y, sent_y, kept_x, sent_x = outer(info, cots, attn_context, far_context, scale, far_scale)
    aways = (x_away, swap(x_away, "c"))
    grad = context_call(context_last_kernel, info, aways, out_weight, (near, part, scale))

    got_y, got_x = swap(sent_y, "y", 1), swap(sent_x, "xh", 1)
    got_y, got_x, grad = lax.optimization_barrier((got_y, got_x, grad))
    second = ring_sum(rest, "z")
    first = jnp.concatenate([kept_y.astype(F32) + got_y.astype(F32), kept_x.astype(F32) + got_x.astype(F32)], -1)
    first = ring_sum(first.astype(BF), "z")
    second = second.reshape(2, 2, 64, REST)
    to_y = jnp.concatenate([second[1, 0], first[1, :, SIDE:]], -1).astype(BF)
    to_x = jnp.concatenate([second[0, 1], first[1, :, :SIDE]], -1).astype(BF)
    both = [(i, i ^ 5) for i in range(8)]
    from_y, from_x = swap(to_y, "y").astype(F32), swap(to_x, "xh").astype(F32)
    from_both = lax.ppermute(second[1, 1].astype(BF), ("xh", "y"), both).astype(F32)
    weight_grad = jnp.concatenate(
        [
            second[0, 0] + from_y[:, :REST] + from_x[:, :REST] + from_both,
            first[0, :, :SIDE] + from_x[:, REST:],
            first[0, :, SIDE:] + from_y[:, REST:],
        ],
        -1,
    )
    return mixture, grad, weight_grad


def solution(mesh):
    split = Mesh(mesh.devices.reshape(8, 2, 4, 2, 2), ALL)
    placed = (P(ALL), P(ALL), P(ALL), P(), P(DP, MP), P(None, MP), P(ALL, None))
    return jax.shard_map(
        work,
        mesh=split,
        in_specs=placed,
        out_specs=(P(), P(DP, MP), P(DP, MP)),
        check_vma=False,
    )
```
